32 devices in a mesh: loop: 8 (over y, x, core), dp: 4 (over z).
Axes of the slice: x: 2, y: 2, z: 4, core: 2. Of those that a mesh axis runs over, the one named last changes fastest.
Arguments:
- codes: bfloat16 [2048, 16, 1024], P(('loop', 'dp')), may hold values from -64 to 64, as said below
- cand_hidden: bfloat16 [2048, 1024], P(('loop', 'dp')), may hold values from -5 to 5, as said below
- proj: bfloat16 [1024, 1024], replicated, may hold values from -1 to 2, as said below
- gold: int32 [2048], P(('loop', 'dp')), may hold values from 0 to 511
Outputs:
- context_loss: float32 [2048], P(('loop', 'dp'))
- code_grad: float32 [2048, 16, 1024], P(('loop', 'dp'))
- proj_grad: float32 [1024, 1024], P(('loop', 'dp'))
The draws below stay inside these ranges and needn't reach their ends.
Inputs may be any that keep to these rules, and one draw needn't show every extreme that they name: codes stay within this range. `cand_hidden`: CLS states stay within this range. `proj`: projection entries stay within this range.
All inputs are finite; a program needn't handle non-finite values.
Results may differ from the reference program's by a relative error of at most 0.0085.
Values may be sent and summed in bfloat16 or wider, within the bound.
A program may use at most 128 MiB of HBM per device.

```python
import math
import jax
import jax.numpy as jnp
from jax import lax

D = 1024
M = 16
B = 64
CONTEXTS = 2048
N_LOOP = 8
N_DP = 4


def base_hidden(key):
    return jnp.clip(jax.random.normal(jax.random.fold_in(key, 7), (CONTEXTS, D), jnp.float32), -5.0, 5.0)


def draw_cand_hidden(key, part):
    return base_hidden(key).astype(jnp.bfloat16)


def draw_proj(key, part):
    noise = jnp.clip(jax.random.normal(jax.random.fold_in(key, 13), (D, D), jnp.float32), -6.0, 6.0)
    matrix = noise / math.sqrt(D)
    return matrix.astype(jnp.bfloat16)


def draw_codes(key, part):
    rough = jnp.clip(jax.random.normal(jax.random.fold_in(key, 21), (CONTEXTS, M, D), jnp.float32), -4.0, 4.0) * 4.0
    return rough.astype(jnp.bfloat16)


def set_ends(drawn, rng, low, top_value):
    place = [jax.random.randint(jax.random.fold_in(rng, axis), (), 0, length) for axis, length in enumerate(drawn.shape)]
    main_axis = drawn.shape.index(max(drawn.shape))
    neighbour = place[:main_axis] + [(place[main_axis] + 1) % drawn.shape[main_axis]] + place[main_axis + 1:]
    return drawn.at[tuple(place)].set(low).at[tuple(neighbour)].set(top_value)


def setup_inputs(seed: int = 0) -> dict:
    arg_keys = jax.random.split(jax.random.key(seed), 5)
    return {
        "codes": draw_codes(jax.random.fold_in(arg_keys[4], 71), 0),
        "cand_hidden": draw_cand_hidden(jax.random.fold_in(arg_keys[4], 71), 0),
        "proj": draw_proj(jax.random.fold_in(arg_keys[4], 71), 0),
        "gold": set_ends(jax.random.randint(arg_keys[3], (CONTEXTS,), 0, B * N_LOOP), jax.random.fold_in(arg_keys[3], 1), 0, (B * N_LOOP) - 1).astype(jnp.int32),
    }


def regroup(array):
    shape = array.shape[1:]
    split = array.reshape((N_LOOP, N_DP, B) + shape)
    moved = jnp.swapaxes(split, 0, 1)
    return moved.reshape((N_DP, N_LOOP * B) + shape)


def ungroup(array):
    shape = array.shape[2:]
    split = array.reshape((N_DP, N_LOOP, B) + shape)
    moved = jnp.swapaxes(split, 0, 1)
    return moved.reshape((N_LOOP * N_DP * B,) + shape)


def reference(codes, cand_hidden, proj, gold):
    inv_scale = D ** -0.5

    def one_group(inputs):
        group_codes, group_hidden, group_gold = inputs
        count = group_hidden.shape[0]
        cand_embed = jnp.dot(group_hidden, proj, preferred_element_type=jnp.float32).astype(jnp.bfloat16)
        code_rows = group_codes.reshape(count * M, D)
        raw = lax.dot_general(cand_embed, code_rows, (((1,), (1,)), ((), ())), preferred_element_type=jnp.float32)
        logits = raw.reshape(count, count, M) * inv_scale
        top_logit = jnp.max(logits, axis=-1, keepdims=True)
        weights = jnp.exp(logits - top_logit)
        probs = weights / jnp.sum(weights, axis=-1, keepdims=True)
        scores = jnp.sum(probs * logits, axis=-1)
        top_score = jnp.max(scores, axis=0)
        log_total = top_score + jnp.log(jnp.sum(jnp.exp(scores - top_score[None, :]), axis=0))
        cand_ids = jnp.arange(count, dtype=jnp.int32)
        gold_hot = (cand_ids[:, None] == group_gold[None, :]).astype(jnp.float32)
        context_loss = log_total - jnp.sum(gold_hot * scores, axis=0)
        score_grad = jnp.exp(scores - log_total[None, :]) - gold_hot
        logit_grad = (score_grad[:, :, None] * probs * (1.0 + logits - scores[:, :, None]) * inv_scale).astype(jnp.bfloat16)
        logit_grad = logit_grad.reshape(count, count * M)
        code_grad = lax.dot_general(logit_grad, cand_embed, (((0,), (0,)), ((), ())), preferred_element_type=jnp.float32)
        embed_grad = jnp.dot(logit_grad, code_rows, preferred_element_type=jnp.float32).astype(jnp.bfloat16)
        proj_part = lax.dot_general(group_hidden, embed_grad, (((0,), (0,)), ((), ())), preferred_element_type=jnp.float32)
        return context_loss, code_grad.reshape(count, M, D), proj_part

    losses, code_grads, proj_parts = lax.map(one_group, (regroup(codes), regroup(cand_hidden), regroup(gold)))
    return ungroup(losses), ungroup(code_grads), jnp.sum(proj_parts, axis=0)
```

```python
import functools

import jax
import jax.numpy as jnp
from jax import lax
from jax.experimental import pallas as pl
from jax.experimental.pallas import tpu as pltpu
from jax.sharding import PartitionSpec as P

MESH = pl.DeviceIdType.MESH
F32 = jnp.float32
BF16 = jnp.bfloat16
LANES = 128
NT = (((1,), (1,)), ((), ()))


def dot(a, b):
    return jnp.dot(a, b, preferred_element_type=F32)


def body(
    ring, groups, ctx, per,
    codes_ref, hidden_ref, proj_ref, gold_ref,
    loss_ref, gradt_ref, embed_ref, out_ref,
    codes, proj, perm, permt, rows, held, logits, scores, grads, hidt,
    e_own, e_sib, e_sum, e_in, p_own, p_in, q_own, q_in,
    local_sem, h_send, h_recv, hs_send, hs_recv, es_send, es_recv,
    ef_send, ef_recv, z_send, z_recv, q_send, q_recv,
):
    width = hidden_ref.shape[1]
    batch = hidden_ref.shape[0]
    chips = ring // 2
    half = chips * batch
    n_rows = ctx * per
    me = lax.axis_index("loop")
    group = lax.axis_index("dp")
    chip, par = me // 2, me % 2
    sibling = chip * 2 + 1 - par
    inv_scale = width ** -0.5

    get_codes = pltpu.make_async_copy(codes_ref, codes, local_sem.at[0])
    get_proj = pltpu.make_async_copy(proj_ref, proj, local_sem.at[1])
    get_hidden = pltpu.make_async_copy(hidden_ref, held.at[par, chip], local_sem.at[2])
    get_hidden.start()
    get_codes.start()
    get_proj.start()

    barrier = pltpu.get_barrier_semaphore()
    for k in range(1, ring):
        pl.semaphore_signal(barrier, 1, device_id={"loop": (me + k) % ring}, device_id_type=MESH)
    for k in range(1, groups):
        pl.semaphore_signal(barrier, 1, device_id={"dp": (group + k) % groups}, device_id_type=MESH)
    get_hidden.wait()
    pl.semaphore_wait(barrier, ring + groups - 2)

    def send(src, dst, ssem, rsem, where):
        copy = pltpu.make_async_remote_copy(
            src_ref=src, dst_ref=dst, send_sem=ssem, recv_sem=rsem,
            device_id=where, device_id_type=MESH)
        copy.start()
        return copy

    pending = []
    far = []
    for k in range(chips - 1):
        to = (chip + 1 + k) % chips
        far.append(send(hidden_ref, held.at[par, chip], h_send.at[k], h_recv.at[k],
                        {"loop": to * 2 + par}))
    near = [send(hidden_ref, held.at[par, chip], hs_send.at[chips - 1], hs_recv.at[chips - 1],
                 {"loop": sibling})]

    row_tile = 128

    @pl.loop(0, n_rows // row_tile)
    def _(t):
        start = pl.multiple_of(t * row_tile, row_tile)
        r = lax.broadcasted_iota(jnp.int32, (row_tile, n_rows), 0) + start
        c = lax.broadcasted_iota(jnp.int32, (row_tile, n_rows), 1)
        perm[pl.ds(start, row_tile), :] = jnp.where(
            c == (r % ctx) * per + r // ctx, 1.0, 0.0).astype(BF16)
        permt[pl.ds(start, row_tile), :] = jnp.where(
            c == (r % per) * ctx + r // per, 1.0, 0.0).astype(BF16)

    get_codes.wait()
    tile = 256

    @pl.loop(0, width // tile)
    def _(t):
        cols = pl.ds(pl.multiple_of(t * tile, tile), tile)
        rows[:, cols] = dot(perm[...], codes[:, cols]).astype(BF16)

    get_proj.wait()
    for k in range(chips - 1):
        far[k].wait_recv()
        src = (chip + chips - 1 - k) % chips
        near.append(send(held.at[par, src], held.at[par, src], hs_send.at[k], hs_recv.at[k],
                         {"loop": sibling}))

    def forward(h):
        mine = pl.ds(pl.multiple_of(h * half, half), half)

        @pl.loop(0, width // tile)
        def _(t):
            cols = pl.ds(pl.multiple_of(t * tile, tile), tile)
            embed_ref[mine, cols] = dot(
                held[h].reshape(half, width), proj[:, cols]).astype(BF16)

        @pl.loop(0, n_rows // tile)
        def _(t):
            cols = pl.ds(pl.multiple_of(t * tile, tile), tile)
            logits[mine, cols] = lax.dot_general(
                embed_ref[mine, :], rows[cols, :], NT,
                preferred_element_type=F32) * inv_scale

        step = 16

        @pl.loop(0, half // step)
        def _(t):
            at = pl.ds(pl.multiple_of(h * half + t * step, step), step)
            parts = [logits[at, j * LANES:(j + 1) * LANES] for j in range(n_rows // LANES)]
            fold = LANES // ctx

            def across(values, op):
                total = functools.reduce(op, values)
                shift = ctx
                while shift < LANES:
                    total = op(total, pltpu.roll(total, shift, axis=1))
                    shift *= 2
                return total

            top = across(parts, jnp.maximum)
            weights = [jnp.exp(x - top) for x in parts]
            inv = 1.0 / across(weights, jnp.add)
            score = across([w * x for w, x in zip(weights, parts)], jnp.add) * inv
            scores[at, :] = score
            for j, (w, x) in enumerate(zip(weights, parts)):
                logits[at, j * LANES:(j + 1) * LANES] = (w * inv) * (1.0 + x - score) * inv_scale

    forward(par)
    for copy in near:
        copy.wait_recv()
    forward(1 - par)

    all_scores = scores[...]
    top_score = jnp.max(all_scores, axis=0, keepdims=True)
    log_total = top_score + jnp.log(jnp.sum(jnp.exp(all_scores - top_score), axis=0, keepdims=True))
    gold = jnp.concatenate([gold_ref[...]] * (LANES // ctx), axis=1)

    def block(b, picked):
        side, c = b // chips, b % chips
        owner = c * 2 + side
        at = pl.ds(pl.multiple_of(b * batch, batch), batch)
        ids = lax.broadcasted_iota(jnp.int32, (batch, LANES), 0) + owner * batch
        hot = jnp.where(ids == gold, 1.0, 0.0)
        score = scores[at, :]
        score_grad = jnp.exp(score - log_total) - hot
        for j in range(n_rows // LANES):
            lanes = slice(j * LANES, (j + 1) * LANES)
            grads[at, lanes] = (score_grad * logits[at, lanes]).astype(BF16)
        return picked + jnp.sum(hot * score, axis=0, keepdims=True)

    picked = lax.fori_loop(0, ring, block, jnp.zeros((1, LANES), F32))
    loss_ref[...] = (log_total - picked)[:, :ctx]

    chunk = width // ring
    sib = []
    for k in range(chips):
        to = (chip + 1 + k) % chips
        cols = pl.ds(pl.multiple_of(to * 2 * chunk, 2 * chunk), 2 * chunk)
        part = dot(grads[...], rows[:, cols]).astype(BF16)
        e_own[k, 0] = part[:, :chunk]
        e_own[k, 1] = part[:, chunk:]
        sib.append(send(e_own.at[k, 1 - par], e_sib.at[k], es_send.at[k], es_recv.at[k],
                        {"loop": sibling}))
    e_far = []
    for k in range(chips):
        to = (chip + 1 + k) % chips
        sib[k].wait_recv()
        total = e_own[k, par].astype(F32) + e_sib[k].astype(F32)
        e_sum[k] = total.astype(BF16)
        if k < chips - 1:
            e_far.append(send(e_sum.at[k], e_in.at[k], ef_send.at[k], ef_recv.at[k],
                              {"loop": to * 2 + par}))

    @pl.loop(0, (2 * half) // tile)
    def _(t):
        cols = pl.ds(pl.multiple_of(t * tile, tile), tile)
        gradt_ref[:, cols] = lax.dot_general(
            permt[...], grads[cols, :], NT, preferred_element_type=F32).astype(BF16)

    hid_all = held.reshape(2 * half, width)

    @pl.loop(0, width // LANES)
    def _(t):
        cols = pl.ds(pl.multiple_of(t * LANES, LANES), LANES)
        hidt[cols, :] = hid_all[:, cols].T

    total = e_sum[chips - 1].astype(F32)
    for k in range(chips - 1):
        e_far[k].wait_recv()
        total = total + e_in[k].astype(F32)
    p_part = dot(hidt[...], total.astype(BF16))
    out_rows = out_ref.shape[0]
    for g in range(groups):
        for l in range(ring):
            first = (l * groups + g) * out_rows
            p_own[g, l] = p_part[first:first + out_rows].astype(BF16)
    z_far = []
    for k in range(groups - 1):
        to = (group + 1 + k) % groups
        z_far.append(send(p_own.at[to], p_in.at[k], z_send.at[k], z_recv.at[k], {"dp": to}))
    total = p_own[group].astype(F32)
    for k in range(groups - 1):
        z_far[k].wait_recv()
        total = total + p_in[k].astype(F32)
    q_own[...] = total.astype(BF16)
    q_far = []
    for k in range(ring - 1):
        to = (me + 1 + k) % ring
        q_far.append(send(q_own.at[to], q_in.at[me], q_send.at[k], q_recv.at[k], {"loop": to}))
    q_in[me] = q_own[me]
    for k in range(ring - 1):
        q_far[k].wait_recv()
    for l in range(ring):
        out_ref[:, l * chunk:(l + 1) * chunk] = q_in[l].astype(F32)
    for copy in far + near + sib + e_far + z_far + q_far:
        copy.wait_send()


def code_body(gradt_ref, embed_ref, out_ref):
    out_ref[...] = dot(gradt_ref[...], embed_ref[...])


def local(ring, groups, codes, cand_hidden, proj, gold):
    ctx, per, width = codes.shape
    batch = cand_hidden.shape[0]
    n_rows = ctx * per
    chips = ring // 2
    cands = ring * batch
    out_rows = width // (ring * groups)
    chunk = width // ring
    vmem = pl.BlockSpec(memory_space=pltpu.VMEM)
    anywhere = pl.BlockSpec(memory_space=pl.ANY)
    dma = pltpu.SemaphoreType.DMA
    loss, gradt, embed, proj_grad = pl.pallas_call(
        functools.partial(body, ring, groups, ctx, per),
        name="link_step",
        out_shape=(
            jax.ShapeDtypeStruct((1, ctx), F32),
            jax.ShapeDtypeStruct((n_rows, cands), BF16),
            jax.ShapeDtypeStruct((cands, width), BF16),
            jax.ShapeDtypeStruct((out_rows, width), F32),
        ),
        in_specs=[anywhere, vmem, anywhere, vmem],
        out_specs=(vmem, vmem, vmem, vmem),
        scratch_shapes=[
            pltpu.VMEM((n_rows, width), BF16),
            pltpu.VMEM((width, width), BF16),
            pltpu.VMEM((n_rows, n_rows), BF16),
            pltpu.VMEM((n_rows, n_rows), BF16),
            pltpu.VMEM((n_rows, width), BF16),
            pltpu.VMEM((2, chips, batch, width), BF16),
            pltpu.VMEM((cands, n_rows), F32),
            pltpu.VMEM((cands, LANES), F32),
            pltpu.VMEM((cands, n_rows), BF16),
            pltpu.VMEM((width, cands), BF16),
            pltpu.VMEM((chips, 2, cands, chunk), BF16),
            pltpu.VMEM((chips, cands, chunk), BF16),
            pltpu.VMEM((chips, cands, chunk), BF16),
            pltpu.VMEM((chips - 1, cands, chunk), BF16),
            pltpu.VMEM((groups, ring, out_rows, chunk), BF16),
            pltpu.VMEM((groups - 1, ring, out_rows, chunk), BF16),
            pltpu.VMEM((ring, out_rows, chunk), BF16),
            pltpu.VMEM((ring, out_rows, chunk), BF16),
            dma((3,)),
            dma((chips - 1,)), dma((chips - 1,)),
            dma((chips,)), dma((chips,)),
            dma((chips,)), dma((chips,)),
            dma((chips - 1,)), dma((chips - 1,)),
            dma((groups - 1,)), dma((groups - 1,)),
            dma((ring - 1,)), dma((ring - 1,)),
        ],
        compiler_params=pltpu.CompilerParams(
            collective_id=0, has_side_effects=True, vmem_limit_bytes=56 * 2**20),
    )(codes.reshape(n_rows, width), cand_hidden, proj, gold.reshape(1, ctx))
    tiles = 4
    code_grad = pl.pallas_call(
        code_body,
        name="code_grad",
        grid=(tiles,),
        out_shape=jax.ShapeDtypeStruct((n_rows, width), F32),
        in_specs=[
            pl.BlockSpec((n_rows // tiles, cands), lambda t: (t, 0)),
            pl.BlockSpec((cands, width), lambda t: (0, 0)),
        ],
        out_specs=pl.BlockSpec((n_rows // tiles, width), lambda t: (t, 0)),
    )(gradt, embed)
    return loss.reshape(ctx), code_grad.reshape(ctx, per, width), proj_grad


def solution(mesh):
    return jax.shard_map(
        functools.partial(local, mesh.shape["loop"], mesh.shape["dp"]),
        mesh=mesh,
        in_specs=(P(("loop", "dp"), None, None), P(("loop", "dp"), None), P(), P(("loop", "dp"))),
        out_specs=(P(("loop", "dp")), P(("loop", "dp"), None, None), P(("loop", "dp"), None)),
        check_vma=False,
    )
```

```python
import functools

import jax
import jax.numpy as jnp
from jax import lax
from jax.experimental import pallas as pl
from jax.experimental.pallas import tpu as pltpu
from jax.sharding import PartitionSpec as P

MESH = pl.DeviceIdType.MESH
F32 = jnp.float32
BF16 = jnp.bfloat16
LANES = 128
STEP = 32
LAG = 1
NT = (((1,), (1,)), ((), ()))


def dot(a, b):
    return jnp.dot(a, b, preferred_element_type=F32)


def body(
    ring, groups, ctx, per,
    codes_ref, hidden_ref, proj_ref, gold_ref,
    loss_ref, gradt_ref, embed_ref, q_in,
    codes, proj, perm, rows, held, embed, logits, slopes, scores, grads, gradt, hidt,
    e_own, e_sib, e_sum, e_in, p_own, p_in, q_own,
    local_sem, h_send, h_recv, hs_send, hs_recv, es_send, es_recv,
    ef_send, ef_recv, z_send, z_recv, q_send, q_recv,
):
    width = hidden_ref.shape[1]
    batch = hidden_ref.shape[0]
    chips = ring // 2
    half = chips * batch
    n_rows = ctx * per
    me = lax.axis_index("loop")
    group = lax.axis_index("dp")
    chip, par = me // 2, me % 2
    sibling = chip * 2 + 1 - par
    inv_scale = width ** -0.5

    get_codes = pltpu.make_async_copy(codes_ref, codes, local_sem.at[0])
    get_proj = pltpu.make_async_copy(proj_ref, proj, local_sem.at[1])
    get_hidden = pltpu.make_async_copy(hidden_ref, held.at[me], local_sem.at[2])
    get_hidden.start()
    get_codes.start()
    get_proj.start()

    barrier = pltpu.get_barrier_semaphore()
    for k in range(1, ring):
        pl.semaphore_signal(barrier, 1, device_id={"loop": (me + k) % ring}, device_id_type=MESH)
    for k in range(1, groups):
        pl.semaphore_signal(barrier, 1, device_id={"dp": (group + k) % groups}, device_id_type=MESH)
    row_tile = 128

    @pl.loop(0, n_rows // row_tile)
    def _(t):
        start = pl.multiple_of(t * row_tile, row_tile)
        r = lax.broadcasted_iota(jnp.int32, (row_tile, n_rows), 0) + start
        c = lax.broadcasted_iota(jnp.int32, (row_tile, n_rows), 1)
        perm[pl.ds(start, row_tile), :] = jnp.where(
            c == (r % ctx) * per + r // ctx, 1.0, 0.0).astype(BF16)

    get_hidden.wait()
    pl.semaphore_wait(barrier, ring + groups - 2)

    def send(src, dst, ssem, rsem, where):
        copy = pltpu.make_async_remote_copy(
            src_ref=src, dst_ref=dst, send_sem=ssem, recv_sem=rsem,
            device_id=where, device_id_type=MESH)
        copy.start()
        return copy

    pending = []
    far = []
    for k in range(chips - 1):
        to = (chip + 1 + k) % chips
        far.append(send(hidden_ref, held.at[me], h_send.at[k], h_recv.at[k],
                        {"loop": to * 2 + par}))
    near = [send(hidden_ref, held.at[me], hs_send.at[chips - 1], hs_recv.at[chips - 1],
                 {"loop": sibling})]

    get_codes.wait()
    tile = 256

    @pl.loop(0, width // tile)
    def _(t):
        cols = pl.ds(pl.multiple_of(t * tile, tile), tile)
        rows[:, cols] = dot(perm[...], codes[:, cols]).astype(BF16)

    get_proj.wait()

    def forward(owners):
        count = len(owners) * batch
        spots = [pl.ds(pl.multiple_of(o * batch, batch), batch) for o in owners]

        @pl.loop(0, width // tile)
        def _(t):
            cols = pl.ds(pl.multiple_of(t * tile, tile), tile)
            part = dot(jnp.concatenate([held[o] for o in owners], axis=0), proj[:, cols])
            for j, spot in enumerate(spots):
                embed[spot, cols] = part[j * batch:(j + 1) * batch].astype(BF16)

        @pl.loop(0, n_rows // tile)
        def _(t):
            cols = pl.ds(pl.multiple_of(t * tile, tile), tile)
            logits[:count, cols] = lax.dot_general(
                jnp.concatenate([embed[spot, :] for spot in spots], axis=0), rows[cols, :], NT,
                preferred_element_type=F32) * inv_scale

        step = STEP
        per_owner = batch // step

        for j, o in enumerate(owners):
            @pl.loop(0, per_owner)
            def _(t):
                src = pl.ds(pl.multiple_of(j * batch + t * step, step), step)
                at = pl.ds(pl.multiple_of(o * batch + t * step, step), step)
                parts = [logits[src, i * LANES:(i + 1) * LANES] for i in range(n_rows // LANES)]

                def across(values, op):
                    while len(values) > 1:
                        values = [op(*values[i:i + 2]) if i + 1 < len(values) else values[i]
                                  for i in range(0, len(values), 2)]
                    total = values[0]
                    shift = ctx
                    while shift < LANES:
                        total = op(total, pltpu.roll(total, shift, axis=1))
                        shift *= 2
                    return total

                top = across(parts, jnp.maximum)
                weights = [jnp.exp(x - top) for x in parts]
                inv = 1.0 / across(weights, jnp.add)
                score = across([w * x for w, x in zip(weights, parts)], jnp.add) * inv
                scores[at, :] = score
                rest = 1.0 - score
                scaled = inv * inv_scale
                for i, (w, x) in enumerate(zip(weights, parts)):
                    slopes[at, i * LANES:(i + 1) * LANES] = (w * scaled) * (x + rest)

    near[0].wait_recv()
    forward([me, sibling])
    mine, theirs = [], []
    for k in range(chips - 1):
        far[k].wait_recv()
        src = (chip + chips - 1 - k) % chips
        near.append(send(held.at[src * 2 + par], held.at[src * 2 + par], hs_send.at[k],
                         hs_recv.at[k], {"loop": sibling}))
        mine.append(src * 2 + par)
        theirs.append(src * 2 + 1 - par)
    forward(mine)
    for copy in near[1:]:
        copy.wait_recv()
    forward(theirs)
    put_embed = pltpu.make_async_copy(embed, embed_ref, local_sem.at[3])
    put_embed.start()

    all_scores = scores[...]
    top_score = jnp.max(all_scores, axis=0, keepdims=True)
    log_total = top_score + jnp.log(jnp.sum(jnp.exp(all_scores - top_score), axis=0, keepdims=True))
    gold = jnp.concatenate([gold_ref[...]] * (LANES // ctx), axis=1)

    def block(b, picked):
        at = pl.ds(pl.multiple_of(b * batch, batch), batch)
        ids = lax.broadcasted_iota(jnp.int32, (batch, LANES), 0) + b * batch
        hot = jnp.where(ids == gold, 1.0, 0.0)
        score = scores[at, :]
        score_grad = jnp.exp(score - log_total) - hot
        for j in range(n_rows // LANES):
            lanes = slice(j * LANES, (j + 1) * LANES)
            grads[at, lanes] = (score_grad * slopes[at, lanes]).astype(BF16)
        return picked + jnp.sum(hot * score, axis=0, keepdims=True)

    picked = lax.fori_loop(0, ring, block, jnp.zeros((1, LANES), F32))
    loss_ref[...] = (log_total - picked)[:, :ctx]

    chunk = width // ring
    sib, e_far = [], []

    def finish(k):
        to = (chip + 1 + k) % chips
        sib[k].wait_recv()
        total = e_own[k, par].astype(F32) + e_sib[k].astype(F32)
        e_sum[k] = total.astype(BF16)
        if k < chips - 1:
            e_far.append(send(e_sum.at[k], e_in.at[k], ef_send.at[k], ef_recv.at[k],
                              {"loop": to * 2 + par}))

    for k in range(chips):
        to = (chip + 1 + k) % chips
        cols = pl.ds(pl.multiple_of(to * 2 * chunk, 2 * chunk), 2 * chunk)
        part = dot(grads[...], rows[:, cols]).astype(BF16)
        e_own[k, 0] = part[:, :chunk]
        e_own[k, 1] = part[:, chunk:]
        sib.append(send(e_own.at[k, 1 - par], e_sib.at[k], es_send.at[k], es_recv.at[k],
                        {"loop": sibling}))
        if k >= LAG:
            finish(k - LAG)
    for k in range(chips - LAG, chips):
        finish(k)

    @pl.loop(0, n_rows // row_tile)
    def _(t):
        start = pl.multiple_of(t * row_tile, row_tile)
        r = lax.broadcasted_iota(jnp.int32, (row_tile, n_rows), 0) + start
        c = lax.broadcasted_iota(jnp.int32, (row_tile, n_rows), 1)
        perm[pl.ds(start, row_tile), :] = jnp.where(
            c == (r % per) * ctx + r // per, 1.0, 0.0).astype(BF16)

    @pl.loop(0, (2 * half) // tile)
    def _(t):
        cols = pl.ds(pl.multiple_of(t * tile, tile), tile)
        gradt[:, cols] = lax.dot_general(
            perm[...], grads[cols, :], NT, preferred_element_type=F32).astype(BF16)

    put_gradt = pltpu.make_async_copy(gradt, gradt_ref, local_sem.at[4])
    put_gradt.start()
    hid_all = held.reshape(2 * half, width)

    @pl.loop(0, width // LANES)
    def _(t):
        cols = pl.ds(pl.multiple_of(t * LANES, LANES), LANES)
        hidt[cols, :] = hid_all[:, cols].T

    total = e_sum[chips - 1].astype(F32)
    for k in range(chips - 1):
        e_far[k].wait_recv()
        total = total + e_in[k].astype(F32)
    p_part = dot(hidt[...], total.astype(BF16))
    out_rows = q_in.shape[1]
    for g in range(groups):
        for l in range(ring):
            first = (l * groups + g) * out_rows
            p_own[g, l] = p_part[first:first + out_rows].astype(BF16)
    z_far = []
    for k in range(groups - 1):
        to = (group + 1 + k) % groups
        z_far.append(send(p_own.at[to], p_in.at[k], z_send.at[k], z_recv.at[k], {"dp": to}))
    total = p_own[group].astype(F32)
    for k in range(groups - 1):
        z_far[k].wait_recv()
        total = total + p_in[k].astype(F32)
    q_own[...] = total.astype(BF16)
    q_far = []
    for k in range(ring - 1):
        to = (me + 1 + k) % ring
        q_far.append(send(q_own.at[to], q_in.at[me], q_send.at[k], q_recv.at[k], {"loop": to}))
    q_in[me] = q_own[me]
    for k in range(ring - 1):
        q_far[k].wait_recv()
    put_embed.wait()
    put_gradt.wait()
    for copy in far + near + sib + e_far + z_far + q_far:
        copy.wait_send()


def code_body(gradt_ref, embed_ref, loss_ref, parts_ref, out_ref, loss_out, proj_out):
    out_ref[...] = dot(gradt_ref[...], embed_ref[...])

    @pl.when(pl.program_id(0) == 0)
    def _():
        chunk = parts_ref.shape[2]
        loss_out[...] = loss_ref[...]
        for l in range(parts_ref.shape[0]):
            proj_out[:, l * chunk:(l + 1) * chunk] = parts_ref[l].astype(F32)


def local(ring, groups, codes, cand_hidden, proj, gold):
    ctx, per, width = codes.shape
    batch = cand_hidden.shape[0]
    n_rows = ctx * per
    chips = ring // 2
    cands = ring * batch
    out_rows = width // (ring * groups)
    chunk = width // ring
    vmem = pl.BlockSpec(memory_space=pltpu.VMEM)
    anywhere = pl.BlockSpec(memory_space=pl.ANY)
    dma = pltpu.SemaphoreType.DMA
    loss, gradt, embed, parts = pl.pallas_call(
        functools.partial(body, ring, groups, ctx, per),
        name="link_step",
        out_shape=(
            jax.ShapeDtypeStruct((1, ctx), F32),
            jax.ShapeDtypeStruct((n_rows, cands), BF16),
            jax.ShapeDtypeStruct((cands, width), BF16),
            jax.ShapeDtypeStruct((ring, out_rows, chunk), BF16),
        ),
        in_specs=[anywhere, vmem, anywhere, vmem],
        out_specs=(vmem, anywhere, anywhere, vmem),
        scratch_shapes=[
            pltpu.VMEM((n_rows, width), BF16),
            pltpu.VMEM((width, width), BF16),
            pltpu.VMEM((n_rows, n_rows), BF16),
            pltpu.VMEM((n_rows, width), BF16),
            pltpu.VMEM((ring, batch, width), BF16),
            pltpu.VMEM((cands, width), BF16),
            pltpu.VMEM((cands, n_rows), F32),
            pltpu.VMEM((cands, n_rows), F32),
            pltpu.VMEM((cands, LANES), F32),
            pltpu.VMEM((cands, n_rows), BF16),
            pltpu.VMEM((n_rows, cands), BF16),
            pltpu.VMEM((width, cands), BF16),
            pltpu.VMEM((chips, 2, cands, chunk), BF16),
            pltpu.VMEM((chips, cands, chunk), BF16),
            pltpu.VMEM((chips, cands, chunk), BF16),
            pltpu.VMEM((chips - 1, cands, chunk), BF16),
            pltpu.VMEM((groups, ring, out_rows, chunk), BF16),
            pltpu.VMEM((groups - 1, ring, out_rows, chunk), BF16),
            pltpu.VMEM((ring, out_rows, chunk), BF16),
            dma((5,)),
            dma((chips - 1,)), dma((chips - 1,)),
            dma((chips,)), dma((chips,)),
            dma((chips,)), dma((chips,)),
            dma((chips - 1,)), dma((chips - 1,)),
            dma((groups - 1,)), dma((groups - 1,)),
            dma((ring - 1,)), dma((ring - 1,)),
        ],
        compiler_params=pltpu.CompilerParams(
            collective_id=0, has_side_effects=True, vmem_limit_bytes=56 * 2**20),
    )(codes.reshape(n_rows, width), cand_hidden, proj, gold.reshape(1, ctx))
    tiles = 4
    code_grad, loss, proj_grad = pl.pallas_call(
        code_body,
        name="code_grad",
        grid=(tiles,),
        out_shape=(
            jax.ShapeDtypeStruct((n_rows, width), F32),
            jax.ShapeDtypeStruct((1, ctx), F32),
            jax.ShapeDtypeStruct((out_rows, width), F32),
        ),
        in_specs=[
            pl.BlockSpec((n_rows // tiles, cands), lambda t: (t, 0)),
            pl.BlockSpec((cands, width), lambda t: (0, 0)),
            pl.BlockSpec((1, ctx), lambda t: (0, 0)),
            pl.BlockSpec((ring, out_rows, chunk), lambda t: (0, 0, 0)),
        ],
        out_specs=(
            pl.BlockSpec((n_rows // tiles, width), lambda t: (t, 0)),
            pl.BlockSpec((1, ctx), lambda t: (0, 0)),
            pl.BlockSpec((out_rows, width), lambda t: (0, 0)),
        ),
    )(gradt, embed, loss, parts)
    return loss.reshape(ctx), code_grad.reshape(ctx, per, width), proj_grad


def solution(mesh):
    return jax.shard_map(
        functools.partial(local, mesh.shape["loop"], mesh.shape["dp"]),
        mesh=mesh,
        in_specs=(P(("loop", "dp"), None, None), P(("loop", "dp"), None), P(), P(("loop", "dp"))),
        out_specs=(P(("loop", "dp")), P(("loop", "dp"), None, None), P(("loop", "dp"), None)),
        check_vma=False,
    )
```

```python
import functools

import jax
import jax.numpy as jnp
from jax import lax
from jax.experimental import pallas as pl
from jax.experimental.pallas import tpu as pltpu
from jax.sharding import PartitionSpec as P

MESH = pl.DeviceIdType.MESH
F32 = jnp.float32
BF16 = jnp.bfloat16
LANES = 128
STEP = 32
LAG = 1
NT = (((1,), (1,)), ((), ()))


def dot(a, b):
    return jnp.dot(a, b, preferred_element_type=F32)


def body(
    ring, groups, ctx, per,
    codes_ref, hidden_ref, proj_ref, gold_ref,
    loss_ref, code_ref, q_in,
    codes, proj, perm, rows, held, embed, logits, slopes, scores, grads, gradt, hidt, code_low,
    e_own, e_sib, e_sum, e_in, p_own, p_in, q_own,
    local_sem, h_send, h_recv, hs_send, hs_recv, es0_send, es0_recv, es_send, es_recv,
    ef_send, ef_recv, z_send, z_recv, q_send, q_recv,
):
    width = hidden_ref.shape[1]
    batch = hidden_ref.shape[0]
    chips = ring // 2
    half = chips * batch
    n_rows = ctx * per
    me = lax.axis_index("loop")
    group = lax.axis_index("dp")
    chip, par = me // 2, me % 2
    sibling = chip * 2 + 1 - par
    inv_scale = width ** -0.5

    get_codes = pltpu.make_async_copy(codes_ref, codes, local_sem.at[0])
    get_proj = pltpu.make_async_copy(proj_ref, proj, local_sem.at[1])
    get_hidden = pltpu.make_async_copy(hidden_ref, held.at[me], local_sem.at[2])
    get_hidden.start()
    get_codes.start()
    get_proj.start()

    barrier = pltpu.get_barrier_semaphore()
    for k in range(1, ring):
        pl.semaphore_signal(barrier, 1, device_id={"loop": (me + k) % ring}, device_id_type=MESH)
    for k in range(1, groups):
        pl.semaphore_signal(barrier, 1, device_id={"dp": (group + k) % groups}, device_id_type=MESH)
    row_tile = 128

    @pl.loop(0, n_rows // row_tile)
    def _(t):
        start = pl.multiple_of(t * row_tile, row_tile)
        r = lax.broadcasted_iota(jnp.int32, (row_tile, n_rows), 0) + start
        c = lax.broadcasted_iota(jnp.int32, (row_tile, n_rows), 1)
        perm[pl.ds(start, row_tile), :] = jnp.where(
            c == (r % ctx) * per + r // ctx, 1.0, 0.0).astype(BF16)

    get_hidden.wait()
    pl.semaphore_wait(barrier, ring + groups - 2)

    def send(src, dst, ssem, rsem, where):
        copy = pltpu.make_async_remote_copy(
            src_ref=src, dst_ref=dst, send_sem=ssem, recv_sem=rsem,
            device_id=where, device_id_type=MESH)
        copy.start()
        return copy

    pending = []
    far = []
    for k in range(chips - 1):
        to = (chip + 1 + k) % chips
        far.append(send(hidden_ref, held.at[me], h_send.at[k], h_recv.at[k],
                        {"loop": to * 2 + par}))
    near = [send(hidden_ref, held.at[me], hs_send.at[chips - 1], hs_recv.at[chips - 1],
                 {"loop": sibling})]

    get_codes.wait()
    tile = 256

    @pl.loop(0, width // tile)
    def _(t):
        cols = pl.ds(pl.multiple_of(t * tile, tile), tile)
        rows[:, cols] = dot(perm[...], codes[:, cols]).astype(BF16)

    get_proj.wait()

    shared = []

    def spots_of(owners):
        return [pl.ds(pl.multiple_of(o * batch, batch), batch) for o in owners]

    def project(owners):
        spots = spots_of(owners)

        @pl.loop(0, width // tile)
        def _(t):
            cols = pl.ds(pl.multiple_of(t * tile, tile), tile)
            part = dot(jnp.concatenate([held[o] for o in owners], axis=0), proj[:, cols])
            for j, spot in enumerate(spots):
                embed[spot, cols] = part[j * batch:(j + 1) * batch].astype(BF16)

        for spot in spots:
            k = len(shared)
            shared.append(send(embed.at[spot], embed.at[spot], es0_send.at[k], es0_recv.at[k],
                               {"loop": sibling}))

    def forward(owners):
        count = len(owners) * batch
        spots = spots_of(owners)

        @pl.loop(0, n_rows // tile)
        def _(t):
            cols = pl.ds(pl.multiple_of(t * tile, tile), tile)
            logits[:count, cols] = lax.dot_general(
                jnp.concatenate([embed[spot, :] for spot in spots], axis=0), rows[cols, :], NT,
                preferred_element_type=F32) * inv_scale

        step = STEP
        per_owner = batch // step

        for j, o in enumerate(owners):
            @pl.loop(0, per_owner)
            def _(t):
                src = pl.ds(pl.multiple_of(j * batch + t * step, step), step)
                at = pl.ds(pl.multiple_of(o * batch + t * step, step), step)
                parts = [logits[src, i * LANES:(i + 1) * LANES] for i in range(n_rows // LANES)]

                def across(values, op):
                    while len(values) > 1:
                        values = [op(*values[i:i + 2]) if i + 1 < len(values) else values[i]
                                  for i in range(0, len(values), 2)]
                    total = values[0]
                    shift = ctx
                    while shift < LANES:
                        total = op(total, pltpu.roll(total, shift, axis=1))
                        shift *= 2
                    return total

                top = across(parts, jnp.maximum)
                weights = [jnp.exp(x - top) for x in parts]
                inv = 1.0 / across(weights, jnp.add)
                score = across([w * x for w, x in zip(weights, parts)], jnp.add) * inv
                scores[at, :] = score
                rest = 1.0 - score
                scaled = inv * inv_scale
                for i, (w, x) in enumerate(zip(weights, parts)):
                    slopes[at, i * LANES:(i + 1) * LANES] = (w * scaled) * (x + rest)

    project([me])
    shared[0].wait_recv()
    forward([me, sibling])
    mine, theirs = [], []
    for k in range(chips - 1):
        far[k].wait_recv()
        src = (chip + chips - 1 - k) % chips
        near.append(send(held.at[src * 2 + par], held.at[src * 2 + par], hs_send.at[k],
                         hs_recv.at[k], {"loop": sibling}))
        mine.append(src * 2 + par)
        theirs.append(src * 2 + 1 - par)
    project(mine)
    forward(mine)
    for copy in shared[1:]:
        copy.wait_recv()
    forward(theirs)

    all_scores = scores[...]
    top_score = jnp.max(all_scores, axis=0, keepdims=True)
    log_total = top_score + jnp.log(jnp.sum(jnp.exp(all_scores - top_score), axis=0, keepdims=True))
    gold = jnp.concatenate([gold_ref[...]] * (LANES // ctx), axis=1)

    def block(b, picked):
        at = pl.ds(pl.multiple_of(b * batch, batch), batch)
        ids = lax.broadcasted_iota(jnp.int32, (batch, LANES), 0) + b * batch
        hot = jnp.where(ids == gold, 1.0, 0.0)
        score = scores[at, :]
        score_grad = jnp.exp(score - log_total) - hot
        for j in range(n_rows // LANES):
            lanes = slice(j * LANES, (j + 1) * LANES)
            grads[at, lanes] = (score_grad * slopes[at, lanes]).astype(BF16)
        return picked + jnp.sum(hot * score, axis=0, keepdims=True)

    picked = lax.fori_loop(0, ring, block, jnp.zeros((1, LANES), F32))
    loss_ref[...] = (log_total - picked)[:, :ctx]

    chunk = width // ring
    sib, e_far = [], []

    def finish(k):
        to = (chip + 1 + k) % chips
        sib[k].wait_recv()
        total = e_own[k, par].astype(F32) + e_sib[k].astype(F32)
        e_sum[k] = total.astype(BF16)
        if k < chips - 1:
            e_far.append(send(e_sum.at[k], e_in.at[k], ef_send.at[k], ef_recv.at[k],
                              {"loop": to * 2 + par}))

    for k in range(chips):
        to = (chip + 1 + k) % chips
        cols = pl.ds(pl.multiple_of(to * 2 * chunk, 2 * chunk), 2 * chunk)
        part = dot(grads[...], rows[:, cols]).astype(BF16)
        e_own[k, 0] = part[:, :chunk]
        e_own[k, 1] = part[:, chunk:]
        sib.append(send(e_own.at[k, 1 - par], e_sib.at[k], es_send.at[k], es_recv.at[k],
                        {"loop": sibling}))
        if k >= LAG:
            finish(k - LAG)
    for k in range(chips - LAG, chips):
        finish(k)

    @pl.loop(0, n_rows // row_tile)
    def _(t):
        start = pl.multiple_of(t * row_tile, row_tile)
        r = lax.broadcasted_iota(jnp.int32, (row_tile, n_rows), 0) + start
        c = lax.broadcasted_iota(jnp.int32, (row_tile, n_rows), 1)
        perm[pl.ds(start, row_tile), :] = jnp.where(
            c == (r % per) * ctx + r // per, 1.0, 0.0).astype(BF16)

    @pl.loop(0, (2 * half) // tile)
    def _(t):
        cols = pl.ds(pl.multiple_of(t * tile, tile), tile)
        gradt[:, cols] = lax.dot_general(
            perm[...], grads[cols, :], NT, preferred_element_type=F32).astype(BF16)

    for copy in near:
        copy.wait_recv()
    hid_all = held.reshape(2 * half, width)

    @pl.loop(0, width // LANES)
    def _(t):
        cols = pl.ds(pl.multiple_of(t * LANES, LANES), LANES)
        hidt[cols, :] = hid_all[:, cols].T

    total = e_sum[chips - 1].astype(F32)
    for k in range(chips - 1):
        e_far[k].wait_recv()
        total = total + e_in[k].astype(F32)
    p_part = dot(hidt[...], total.astype(BF16))
    out_rows = q_in.shape[1]
    for g in range(groups):
        for l in range(ring):
            first = (l * groups + g) * out_rows
            p_own[g, l] = p_part[first:first + out_rows].astype(BF16)
    z_far = []
    for k in range(groups - 1):
        to = (group + 1 + k) % groups
        z_far.append(send(p_own.at[to], p_in.at[k], z_send.at[k], z_recv.at[k], {"dp": to}))
    @pl.loop(0, n_rows // tile)
    def _(t):
        at = pl.ds(pl.multiple_of(t * tile, tile), tile)
        code_low[at, :] = dot(gradt[at, :], embed[...]).astype(BF16)

    put_code = pltpu.make_async_copy(code_low, code_ref, local_sem.at[3])
    put_code.start()
    total = p_own[group].astype(F32)
    for k in range(groups - 1):
        z_far[k].wait_recv()
        total = total + p_in[k].astype(F32)
    q_own[...] = total.astype(BF16)
    q_far = []
    for k in range(ring - 1):
        to = (me + 1 + k) % ring
        q_far.append(send(q_own.at[to], q_in.at[me], q_send.at[k], q_recv.at[k], {"loop": to}))
    q_in[me] = q_own[me]
    for k in range(ring - 1):
        q_far[k].wait_recv()
    put_code.wait()
    for copy in far + near + shared + sib + e_far + z_far + q_far:
        copy.wait_send()


def code_body(code_ref, loss_ref, parts_ref, out_ref, loss_out, proj_out):
    out_ref[...] = code_ref[...].astype(F32)

    @pl.when(pl.program_id(0) == 0)
    def _():
        chunk = parts_ref.shape[2]
        loss_out[...] = loss_ref[...]
        for l in range(parts_ref.shape[0]):
            proj_out[:, l * chunk:(l + 1) * chunk] = parts_ref[l].astype(F32)


def local(ring, groups, codes, cand_hidden, proj, gold):
    ctx, per, width = codes.shape
    batch = cand_hidden.shape[0]
    n_rows = ctx * per
    chips = ring // 2
    cands = ring * batch
    out_rows = width // (ring * groups)
    chunk = width // ring
    vmem = pl.BlockSpec(memory_space=pltpu.VMEM)
    anywhere = pl.BlockSpec(memory_space=pl.ANY)
    dma = pltpu.SemaphoreType.DMA
    loss, code_low, parts = pl.pallas_call(
        functools.partial(body, ring, groups, ctx, per),
        name="link_step",
        out_shape=(
            jax.ShapeDtypeStruct((1, ctx), F32),
            jax.ShapeDtypeStruct((n_rows, width), BF16),
            jax.ShapeDtypeStruct((ring, out_rows, chunk), BF16),
        ),
        in_specs=[anywhere, vmem, anywhere, vmem],
        out_specs=(vmem, anywhere, vmem),
        scratch_shapes=[
            pltpu.VMEM((n_rows, width), BF16),
            pltpu.VMEM((width, width), BF16),
            pltpu.VMEM((n_rows, n_rows), BF16),
            pltpu.VMEM((n_rows, width), BF16),
            pltpu.VMEM((ring, batch, width), BF16),
            pltpu.VMEM((cands, width), BF16),
            pltpu.VMEM((cands, n_rows), F32),
            pltpu.VMEM((cands, n_rows), F32),
            pltpu.VMEM((cands, LANES), F32),
            pltpu.VMEM((cands, n_rows), BF16),
            pltpu.VMEM((n_rows, cands), BF16),
            pltpu.VMEM((width, cands), BF16),
            pltpu.VMEM((n_rows, width), BF16),
            pltpu.VMEM((chips, 2, cands, chunk), BF16),
            pltpu.VMEM((chips, cands, chunk), BF16),
            pltpu.VMEM((chips, cands, chunk), BF16),
            pltpu.VMEM((chips - 1, cands, chunk), BF16),
            pltpu.VMEM((groups, ring, out_rows, chunk), BF16),
            pltpu.VMEM((groups - 1, ring, out_rows, chunk), BF16),
            pltpu.VMEM((ring, out_rows, chunk), BF16),
            dma((4,)),
            dma((chips - 1,)), dma((chips - 1,)),
            dma((chips,)), dma((chips,)),
            dma((chips,)), dma((chips,)),
            dma((chips,)), dma((chips,)),
            dma((chips - 1,)), dma((chips - 1,)),
            dma((groups - 1,)), dma((groups - 1,)),
            dma((ring - 1,)), dma((ring - 1,)),
        ],
        compiler_params=pltpu.CompilerParams(
            collective_id=0, has_side_effects=True, vmem_limit_bytes=56 * 2**20),
    )(codes.reshape(n_rows, width), cand_hidden, proj, gold.reshape(1, ctx))
    tiles = 4
    code_grad, loss, proj_grad = pl.pallas_call(
        code_body,
        name="code_grad",
        grid=(tiles,),
        out_shape=(
            jax.ShapeDtypeStruct((n_rows, width), F32),
            jax.ShapeDtypeStruct((1, ctx), F32),
            jax.ShapeDtypeStruct((out_rows, width), F32),
        ),
        in_specs=[
            pl.BlockSpec((n_rows // tiles, width), lambda t: (t, 0)),
            pl.BlockSpec((1, ctx), lambda t: (0, 0)),
            pl.BlockSpec((ring, out_rows, chunk), lambda t: (0, 0, 0)),
        ],
        out_specs=(
            pl.BlockSpec((n_rows // tiles, width), lambda t: (t, 0)),
            pl.BlockSpec((1, ctx), lambda t: (0, 0)),
            pl.BlockSpec((out_rows, width), lambda t: (0, 0)),
        ),
    )(code_low, loss, parts)
    return loss.reshape(ctx), code_grad.reshape(ctx, per, width), proj_grad


def solution(mesh):
    return jax.shard_map(
        functools.partial(local, mesh.shape["loop"], mesh.shape["dp"]),
        mesh=mesh,
        in_specs=(P(("loop", "dp"), None, None), P(("loop", "dp"), None), P(), P(("loop", "dp"))),
        out_specs=(P(("loop", "dp")), P(("loop", "dp"), None, None), P(("loop", "dp"), None)),
        check_vma=False,
    )
```

```python
import functools

import jax
import jax.numpy as jnp
from jax import lax
from jax.experimental import pallas as pl
from jax.experimental.pallas import tpu as pltpu
from jax.sharding import PartitionSpec as P

MESH = pl.DeviceIdType.MESH
F32 = jnp.float32
BF16 = jnp.bfloat16
LANES = 128
STEP = 64
LAG = 1
NT = (((1,), (1,)), ((), ()))


def dot(a, b):
    return jnp.dot(a, b, preferred_element_type=F32)


def body(
    ring, groups, ctx, per,
    codes_ref, hidden_ref, proj_ref, gold_ref,
    loss_ref, code_ref, q_in,
    codes, proj, perm, rows, held, embed, logits, slopes, scores, grads, gradt, hidt, code_low,
    e_own, e_sib, e_sum, e_in, p_own, p_in, q_own,
    local_sem, h_send, h_recv, hs_send, hs_recv, es0_send, es0_recv, es_send, es_recv,
    ef_send, ef_recv, z_send, z_recv, q_send, q_recv,
):
    width = hidden_ref.shape[1]
    batch = hidden_ref.shape[0]
    chips = ring // 2
    half = chips * batch
    n_rows = ctx * per
    me = lax.axis_index("loop")
    group = lax.axis_index("dp")
    chip, par = me // 2, me % 2
    sibling = chip * 2 + 1 - par
    inv_scale = width ** -0.5

    get_codes = pltpu.make_async_copy(codes_ref, codes, local_sem.at[0])
    get_proj = pltpu.make_async_copy(proj_ref, proj, local_sem.at[1])
    get_hidden = pltpu.make_async_copy(hidden_ref, held.at[me], local_sem.at[2])
    get_hidden.start()
    get_codes.start()
    get_proj.start()

    barrier = pltpu.get_barrier_semaphore()
    for k in range(1, ring):
        pl.semaphore_signal(barrier, 1, device_id={"loop": (me + k) % ring}, device_id_type=MESH)
    for k in range(1, groups):
        pl.semaphore_signal(barrier, 1, device_id={"dp": (group + k) % groups}, device_id_type=MESH)
    row_tile = 128

    @pl.loop(0, n_rows // row_tile)
    def _(t):
        start = pl.multiple_of(t * row_tile, row_tile)
        r = lax.broadcasted_iota(jnp.int32, (row_tile, n_rows), 0) + start
        c = lax.broadcasted_iota(jnp.int32, (row_tile, n_rows), 1)
        perm[pl.ds(start, row_tile), :] = jnp.where(
            c == (r % ctx) * per + r // ctx, 1.0, 0.0).astype(BF16)

    get_hidden.wait()
    pl.semaphore_wait(barrier, ring + groups - 2)

    def send(src, dst, ssem, rsem, where):
        copy = pltpu.make_async_remote_copy(
            src_ref=src, dst_ref=dst, send_sem=ssem, recv_sem=rsem,
            device_id=where, device_id_type=MESH)
        copy.start()
        return copy

    pending = []
    far = []
    for k in range(chips - 1):
        to = (chip + 1 + k) % chips
        far.append(send(hidden_ref, held.at[me], h_send.at[k], h_recv.at[k],
                        {"loop": to * 2 + par}))
    near = [send(hidden_ref, held.at[me], hs_send.at[chips - 1], hs_recv.at[chips - 1],
                 {"loop": sibling})]

    get_codes.wait()
    tile = 256

    @pl.loop(0, width // tile)
    def _(t):
        cols = pl.ds(pl.multiple_of(t * tile, tile), tile)
        rows[:, cols] = dot(perm[...], codes[:, cols]).astype(BF16)

    get_proj.wait()

    shared = []

    def spots_of(owners):
        return [pl.ds(pl.multiple_of(o * batch, batch), batch) for o in owners]

    def project(owners):
        spots = spots_of(owners)

        @pl.loop(0, width // tile)
        def _(t):
            cols = pl.ds(pl.multiple_of(t * tile, tile), tile)
            part = dot(jnp.concatenate([held[o] for o in owners], axis=0), proj[:, cols])
            for j, spot in enumerate(spots):
                embed[spot, cols] = part[j * batch:(j + 1) * batch].astype(BF16)

        for spot in spots:
            k = len(shared)
            shared.append(send(embed.at[spot], embed.at[spot], es0_send.at[k], es0_recv.at[k],
                               {"loop": sibling}))

    def forward(owners):
        count = len(owners) * batch
        spots = spots_of(owners)

        @pl.loop(0, n_rows // tile)
        def _(t):
            cols = pl.ds(pl.multiple_of(t * tile, tile), tile)
            logits[:count, cols] = lax.dot_general(
                jnp.concatenate([embed[spot, :] for spot in spots], axis=0), rows[cols, :], NT,
                preferred_element_type=F32) * inv_scale

        step = STEP
        per_owner = batch // step

        for j, o in enumerate(owners):
            @pl.loop(0, per_owner)
            def _(t):
                src = pl.ds(pl.multiple_of(j * batch + t * step, step), step)
                at = pl.ds(pl.multiple_of(o * batch + t * step, step), step)
                parts = [logits[src, i * LANES:(i + 1) * LANES] for i in range(n_rows // LANES)]

                def across(values, op):
                    while len(values) > 1:
                        values = [op(*values[i:i + 2]) if i + 1 < len(values) else values[i]
                                  for i in range(0, len(values), 2)]
                    total = values[0]
                    shift = ctx
                    while shift < LANES:
                        total = op(total, pltpu.roll(total, shift, axis=1))
                        shift *= 2
                    return total

                top = across(parts, jnp.maximum)
                weights = [jnp.exp(x - top) for x in parts]
                inv = 1.0 / across(weights, jnp.add)
                score = across([w * x for w, x in zip(weights, parts)], jnp.add) * inv
                scores[at, :] = score
                rest = 1.0 - score
                scaled = inv * inv_scale
                for i, (w, x) in enumerate(zip(weights, parts)):
                    slopes[at, i * LANES:(i + 1) * LANES] = (w * scaled) * (x + rest)

    project([me])
    shared[0].wait_recv()
    forward([me, sibling])
    mine, theirs = [], []
    for k in range(chips - 1):
        far[k].wait_recv()
        src = (chip + chips - 1 - k) % chips
        near.append(send(held.at[src * 2 + par], held.at[src * 2 + par], hs_send.at[k],
                         hs_recv.at[k], {"loop": sibling}))
        mine.append(src * 2 + par)
        theirs.append(src * 2 + 1 - par)
    project(mine)
    forward(mine)
    for copy in shared[1:]:
        copy.wait_recv()
    forward(theirs)

    all_scores = scores[...]
    top_score = jnp.max(all_scores, axis=0, keepdims=True)
    log_total = top_score + jnp.log(jnp.sum(jnp.exp(all_scores - top_score), axis=0, keepdims=True))
    gold = jnp.concatenate([gold_ref[...]] * (LANES // ctx), axis=1)

    def block(b, picked):
        at = pl.ds(pl.multiple_of(b * batch, batch), batch)
        ids = lax.broadcasted_iota(jnp.int32, (batch, LANES), 0) + b * batch
        hot = jnp.where(ids == gold, 1.0, 0.0)
        score = scores[at, :]
        score_grad = jnp.exp(score - log_total) - hot
        for j in range(n_rows // LANES):
            lanes = slice(j * LANES, (j + 1) * LANES)
            grads[at, lanes] = (score_grad * slopes[at, lanes]).astype(BF16)
        return picked + jnp.sum(hot * score, axis=0, keepdims=True)

    picked = lax.fori_loop(0, ring, block, jnp.zeros((1, LANES), F32))
    loss_ref[...] = (log_total - picked)[:, :ctx]

    chunk = width // ring
    sib, e_far = [], []

    def finish(k):
        to = (chip + 1 + k) % chips
        sib[k].wait_recv()
        total = e_own[k, par].astype(F32) + e_sib[k].astype(F32)
        e_sum[k] = total.astype(BF16)
        if k < chips - 1:
            e_far.append(send(e_sum.at[k], e_in.at[k], ef_send.at[k], ef_recv.at[k],
                              {"loop": to * 2 + par}))

    for k in range(chips):
        to = (chip + 1 + k) % chips
        cols = pl.ds(pl.multiple_of(to * 2 * chunk, 2 * chunk), 2 * chunk)
        part = dot(grads[...], rows[:, cols]).astype(BF16)
        e_own[k, 0] = part[:, :chunk]
        e_own[k, 1] = part[:, chunk:]
        sib.append(send(e_own.at[k, 1 - par], e_sib.at[k], es_send.at[k], es_recv.at[k],
                        {"loop": sibling}))
        if k >= LAG:
            finish(k - LAG)
    for k in range(chips - LAG, chips):
        finish(k)

    @pl.loop(0, n_rows // row_tile)
    def _(t):
        start = pl.multiple_of(t * row_tile, row_tile)
        r = lax.broadcasted_iota(jnp.int32, (row_tile, n_rows), 0) + start
        c = lax.broadcasted_iota(jnp.int32, (row_tile, n_rows), 1)
        perm[pl.ds(start, row_tile), :] = jnp.where(
            c == (r % per) * ctx + r // per, 1.0, 0.0).astype(BF16)

    @pl.loop(0, (2 * half) // tile)
    def _(t):
        cols = pl.ds(pl.multiple_of(t * tile, tile), tile)
        gradt[:, cols] = lax.dot_general(
            perm[...], grads[cols, :], NT, preferred_element_type=F32).astype(BF16)

    for copy in near:
        copy.wait_recv()
    hid_all = held.reshape(2 * half, width)

    @pl.loop(0, width // LANES)
    def _(t):
        cols = pl.ds(pl.multiple_of(t * LANES, LANES), LANES)
        hidt[cols, :] = hid_all[:, cols].T

    total = e_sum[chips - 1].astype(F32)
    for k in range(chips - 1):
        e_far[k].wait_recv()
        total = total + e_in[k].astype(F32)
    p_part = dot(hidt[...], total.astype(BF16))
    out_rows = q_in.shape[1]
    for g in range(groups):
        for l in range(ring):
            first = (l * groups + g) * out_rows
            p_own[g, l] = p_part[first:first + out_rows].astype(BF16)
    z_far = []
    for k in range(groups - 1):
        to = (group + 1 + k) % groups
        z_far.append(send(p_own.at[to], p_in.at[k], z_send.at[k], z_recv.at[k], {"dp": to}))
    @pl.loop(0, n_rows // tile)
    def _(t):
        at = pl.ds(pl.multiple_of(t * tile, tile), tile)
        code_low[at, :] = dot(gradt[at, :], embed[...]).astype(BF16)

    put_code = pltpu.make_async_copy(code_low, code_ref, local_sem.at[3])
    put_code.start()
    total = p_own[group].astype(F32)
    for k in range(groups - 1):
        z_far[k].wait_recv()
        total = total + p_in[k].astype(F32)
    q_own[...] = total.astype(BF16)
    q_far = []
    for k in range(ring - 1):
        to = (me + 1 + k) % ring
        q_far.append(send(q_own.at[to], q_in.at[me], q_send.at[k], q_recv.at[k], {"loop": to}))
    q_in[me] = q_own[me]
    for k in range(ring - 1):
        q_far[k].wait_recv()
    put_code.wait()
    for copy in far + near + shared + sib + e_far + z_far + q_far:
        copy.wait_send()


def code_body(code_ref, loss_ref, parts_ref, out_ref, loss_out, proj_out):
    out_ref[...] = code_ref[...].astype(F32)

    @pl.when(pl.program_id(0) == 0)
    def _():
        chunk = parts_ref.shape[2]
        loss_out[...] = loss_ref[...]
        for l in range(parts_ref.shape[0]):
            proj_out[:, l * chunk:(l + 1) * chunk] = parts_ref[l].astype(F32)


def local(ring, groups, codes, cand_hidden, proj, gold):
    ctx, per, width = codes.shape
    batch = cand_hidden.shape[0]
    n_rows = ctx * per
    chips = ring // 2
    cands = ring * batch
    out_rows = width // (ring * groups)
    chunk = width // ring
    vmem = pl.BlockSpec(memory_space=pltpu.VMEM)
    anywhere = pl.BlockSpec(memory_space=pl.ANY)
    dma = pltpu.SemaphoreType.DMA
    loss, code_low, parts = pl.pallas_call(
        functools.partial(body, ring, groups, ctx, per),
        name="link_step",
        out_shape=(
            jax.ShapeDtypeStruct((1, ctx), F32),
            jax.ShapeDtypeStruct((n_rows, width), BF16),
            jax.ShapeDtypeStruct((ring, out_rows, chunk), BF16),
        ),
        in_specs=[anywhere, vmem, anywhere, vmem],
        out_specs=(vmem, anywhere, vmem),
        scratch_shapes=[
            pltpu.VMEM((n_rows, width), BF16),
            pltpu.VMEM((width, width), BF16),
            pltpu.VMEM((n_rows, n_rows), BF16),
            pltpu.VMEM((n_rows, width), BF16),
            pltpu.VMEM((ring, batch, width), BF16),
            pltpu.VMEM((cands, width), BF16),
            pltpu.VMEM((cands, n_rows), F32),
            pltpu.VMEM((cands, n_rows), F32),
            pltpu.VMEM((cands, LANES), F32),
            pltpu.VMEM((cands, n_rows), BF16),
            pltpu.VMEM((n_rows, cands), BF16),
            pltpu.VMEM((width, cands), BF16),
            pltpu.VMEM((n_rows, width), BF16),
            pltpu.VMEM((chips, 2, cands, chunk), BF16),
            pltpu.VMEM((chips, cands, chunk), BF16),
            pltpu.VMEM((chips, cands, chunk), BF16),
            pltpu.VMEM((chips - 1, cands, chunk), BF16),
            pltpu.VMEM((groups, ring, out_rows, chunk), BF16),
            pltpu.VMEM((groups - 1, ring, out_rows, chunk), BF16),
            pltpu.VMEM((ring, out_rows, chunk), BF16),
            dma((4,)),
            dma((chips - 1,)), dma((chips - 1,)),
            dma((chips,)), dma((chips,)),
            dma((chips,)), dma((chips,)),
            dma((chips,)), dma((chips,)),
            dma((chips - 1,)), dma((chips - 1,)),
            dma((groups - 1,)), dma((groups - 1,)),
            dma((ring - 1,)), dma((ring - 1,)),
        ],
        compiler_params=pltpu.CompilerParams(
            collective_id=0, has_side_effects=True, vmem_limit_bytes=56 * 2**20),
    )(codes.reshape(n_rows, width), cand_hidden, proj, gold.reshape(1, ctx))
    tiles = 2
    code_grad, loss, proj_grad = pl.pallas_call(
        code_body,
        name="code_grad",
        grid=(tiles,),
        out_shape=(
            jax.ShapeDtypeStruct((n_rows, width), F32),
            jax.ShapeDtypeStruct((1, ctx), F32),
            jax.ShapeDtypeStruct((out_rows, width), F32),
        ),
        in_specs=[
            pl.BlockSpec((n_rows // tiles, width), lambda t: (t, 0)),
            pl.BlockSpec((1, ctx), lambda t: (0, 0)),
            pl.BlockSpec((ring, out_rows, chunk), lambda t: (0, 0, 0)),
        ],
        out_specs=(
            pl.BlockSpec((n_rows // tiles, width), lambda t: (t, 0)),
            pl.BlockSpec((1, ctx), lambda t: (0, 0)),
            pl.BlockSpec((out_rows, width), lambda t: (0, 0)),
        ),
    )(code_low, loss, parts)
    return loss.reshape(ctx), code_grad.reshape(ctx, per, width), proj_grad


def solution(mesh):
    return jax.shard_map(
        functools.partial(local, mesh.shape["loop"], mesh.shape["dp"]),
        mesh=mesh,
        in_specs=(P(("loop", "dp"), None, None), P(("loop", "dp"), None), P(), P(("loop", "dp"))),
        out_specs=(P(("loop", "dp")), P(("loop", "dp"), None, None), P(("loop", "dp"), None)),
        check_vma=False,
    )
```
